256 devices in a mesh: ctx: 32 (over y, z), chan: 8 (over x, core).
Axes of the slice: x: 4, y: 4, z: 8, core: 2. Of those that a mesh axis runs over, the one named last changes fastest.
Arguments:
- layer_in: float32 [4096, 8192], P('ctx', 'chan'), may hold values from -64 to 64
- query_mr: float32 [4096, 8192], P('ctx', 'chan'), may hold values from -6 to 6
- key_mr: float32 [4096, 8192], P('ctx', 'chan'), may hold values from -6 to 6
- query_lr: float32 [4096, 8192], P('ctx', 'chan'), may hold values from -6 to 6
- key_lr: float32 [4096, 8192], P('ctx', 'chan'), may hold values from -6 to 6
- filter_mr: float32 [128, 8192], P(None, 'chan'), may hold values from -0.5 to 0.5
- filter_lr: float32 [4096, 8192], P('ctx', 'chan'), may hold values from -0.09375 to 0.09375
- norm_gain: float32 [8192], P('chan'), may hold values from 0.1 to 1.9
- out_grad: float32 [4096, 8192], P('ctx', 'chan'), may hold values from -6 to 6
Outputs:
- grad_in: float32 [4096, 8192], P('ctx', 'chan')
- grad_query_mr: float32 [4096, 8192], P('ctx', 'chan')
- grad_key_mr: float32 [4096, 8192], P('ctx', 'chan')
- grad_filter_mr: float32 [128, 8192], P(None, 'chan')
- grad_gain: float32 [8192], P('chan')
- grad_query_lr: float32 [4096, 8192], P('ctx', 'chan')
- grad_key_lr: float32 [4096, 8192], P('ctx', 'chan')
- grad_filter_lr: float32 [4096, 8192], P('ctx', 'chan')
The draws below stay inside these ranges and needn't reach their ends.
All inputs are finite; a program needn't handle non-finite values.
Results may differ from the reference program's by a relative error of at most 0.0003.
Values sent between devices are 32-bit elements; how exact they have to be, the bound alone decides.
No kernel may reach another device: no remote copies, remote signals or barrier semaphores. Data moves between devices by JAX's collectives and lax.ppermute only.
A program may use at most 64 MiB of HBM per device.

```python
import math
import jax
import jax.numpy as jnp
from jax import lax

D = 8192
TAPS = 128
TOKENS = 4096


def draw_layer_in(key, part):
    key_base = jax.random.fold_in(key, 11)
    key_rows = jax.random.fold_in(key, 12)
    key_cols = jax.random.fold_in(key, 13)
    base = jnp.clip(jax.random.normal(key_base, (TOKENS, D), jnp.float32), -6.0, 6.0)
    row_scale = jnp.exp(jax.random.uniform(key_rows, (TOKENS, 1), jnp.float32, math.log(0.3), math.log(3.0)))
    ramp = jnp.arange(D, dtype=jnp.float32) / D
    col_scale = jnp.exp(math.log(3.0) * (ramp - 0.5) + jax.random.uniform(key_cols, (D,), jnp.float32, -0.6, 0.6))
    return base * row_scale * col_scale[None, :]


def block_levels(stream_key, shape, cuts, low, top_value):
    loudness, own = 1.0, jax.random.fold_in(stream_key, 6)
    for position, parts in cuts:
        draws = jnp.exp(jax.random.uniform(jax.random.fold_in(own, position), (parts,), jnp.float32, low / len(cuts), top_value / len(cuts)))
        loudness = loudness * jnp.repeat(draws, shape[position] // parts).reshape([-1 if axis == position else 1 for axis in range(len(shape))])
    return loudness


def gaussian(stream_key, shape, width, most, shards=(), kind=jnp.bfloat16):
    level = block_levels(stream_key, shape, shards, -0.22, 0.18) if shards else 1.0
    values = jax.random.normal(stream_key, shape, jnp.float32) * width * level
    return jnp.minimum(jnp.maximum(values, -most), most).astype(kind)


def setup_inputs(seed: int = 0) -> dict:
    streams_of = jax.random.split(jax.random.key(seed), 10)
    return {
        "layer_in": draw_layer_in(jax.random.fold_in(streams_of[9], 71), 0),
        "query_mr": gaussian(streams_of[1], (TOKENS, D), 1.0, 6.0, ((0, 32), (1, 8)), jnp.float32),
        "key_mr": gaussian(streams_of[2], (TOKENS, D), 1.0, 6.0, ((0, 32), (1, 8)), jnp.float32),
        "query_lr": gaussian(streams_of[3], (TOKENS, D), 1.0, 6.0, ((0, 32), (1, 8)), jnp.float32),
        "key_lr": gaussian(streams_of[4], (TOKENS, D), 1.0, 6.0, ((0, 32), (1, 8)), jnp.float32),
        "filter_mr": gaussian(streams_of[5], (TAPS, D), TAPS ** -0.5, 0.5, ((1, 8),), jnp.float32),
        "filter_lr": gaussian(streams_of[6], (TOKENS, D), TOKENS ** -0.5, 0.09375, ((0, 32), (1, 8)), jnp.float32),
        "norm_gain": jnp.clip(1.0 + 0.18 * jax.random.normal(streams_of[7], (D,), jnp.float32), 0.1, 1.9),
        "out_grad": gaussian(streams_of[8], (TOKENS, D), 1.0, 6.0, ((0, 32), (1, 8)), jnp.float32),
    }


def causal_taps(extended, kernel, length):
    tap_count = kernel.shape[0]

    def add_tap(index, total):
        start = (tap_count - 1 - index).astype(jnp.int32)
        window = lax.dynamic_slice_in_dim(extended, start, length, 0)
        weight = lax.dynamic_slice_in_dim(kernel, index.astype(jnp.int32), 1, 0)
        return total + weight * window
    zeros = jnp.zeros((length, extended.shape[1]), jnp.float32)
    return lax.fori_loop(jnp.int32(0), jnp.int32(tap_count), add_tap, zeros)

def anti_taps(extended, kernel, length):
    tap_count = kernel.shape[0]

    def add_tap(index, total):
        window = lax.dynamic_slice_in_dim(extended, index.astype(jnp.int32), length, 0)
        weight = lax.dynamic_slice_in_dim(kernel, index.astype(jnp.int32), 1, 0)
        return total + weight * window
    zeros = jnp.zeros((length, extended.shape[1]), jnp.float32)
    return lax.fori_loop(jnp.int32(0), jnp.int32(tap_count), add_tap, zeros)

def tap_products(extended, grads, tap_count):
    length = grads.shape[0]

    def one_tap(index):
        start = (tap_count - 1 - index).astype(jnp.int32)
        window = lax.dynamic_slice_in_dim(extended, start, length, 0)
        return lax.optimization_barrier(jnp.sum(grads * window, axis=0))
    return lax.map(one_tap, jnp.arange(tap_count, dtype=jnp.int32))

def long_block(pieces):
    values, grad_pieces, filt_piece = pieces
    length = values.shape[1]
    padded = 2 * length
    spec_values = jnp.fft.rfft(values, n=padded, axis=1)
    spec_grads = jnp.fft.rfft(grad_pieces, n=padded, axis=1)
    spec_filter = jnp.fft.rfft(filt_piece, n=padded, axis=1)
    conv_full = jnp.fft.irfft(spec_values * spec_filter, n=padded, axis=1)[:, :length]
    back_full = jnp.fft.irfft(jnp.conj(spec_filter) * spec_grads, n=padded, axis=1)[:, :length]
    filter_full = jnp.fft.irfft(jnp.conj(spec_values) * spec_grads, n=padded, axis=1)[:, :length]
    return (conv_full, back_full, filter_full)

def reference(layer_in, query_mr, key_mr, query_lr, key_lr, filter_mr, filter_lr, norm_gain, out_grad):
    block_width = math.gcd(D, 256)

    def by_blocks(array):
        return array.T.reshape(D // block_width, block_width, TOKENS)

    def from_blocks(array):
        return array.reshape(D, TOKENS).T
    mixed_in = key_mr * layer_in
    mixed_ext = jnp.concatenate([jnp.zeros((TAPS - 1, D), jnp.float32), mixed_in], 0)
    conv_mr = causal_taps(mixed_ext, filter_mr, TOKENS)
    residual = layer_in + query_mr * conv_mr
    inv_rms = lax.rsqrt(lax.optimization_barrier(jnp.mean(residual * residual, axis=1)) + 1e-06)[:, None]
    normed = residual * inv_rms * norm_gain
    long_in = key_lr * normed
    grad_conv_lr = out_grad * query_lr
    conv_b, back_b, filt_b = lax.map(long_block, (by_blocks(long_in), by_blocks(grad_conv_lr), by_blocks(filter_lr)))
    conv_lr = from_blocks(conv_b)
    grad_long_in = from_blocks(back_b)
    grad_filter_lr = from_blocks(filt_b)
    grad_query_lr = out_grad * conv_lr
    grad_key_lr = grad_long_in * normed
    grad_normed = grad_long_in * key_lr
    grad_gain = lax.optimization_barrier(jnp.sum(grad_normed * residual * inv_rms, axis=0))
    scaled = norm_gain * grad_normed
    cross_mean = lax.optimization_barrier(jnp.mean(scaled * residual, axis=1))[:, None]
    grad_resid = out_grad + inv_rms * scaled - residual * inv_rms ** 3 * cross_mean
    grad_query_mr = grad_resid * conv_mr
    grad_conv_mr = grad_resid * query_mr
    grad_filter_mr = tap_products(mixed_ext, grad_conv_mr, TAPS)
    grad_ext = jnp.concatenate([grad_conv_mr, jnp.zeros((TAPS - 1, D), jnp.float32)], 0)
    grad_mixed = anti_taps(grad_ext, filter_mr, TOKENS)
    grad_key_mr = grad_mixed * layer_in
    grad_in = grad_resid + grad_mixed * key_mr
    return (grad_in, grad_query_mr, grad_key_mr, grad_filter_mr, grad_gain, grad_query_lr, grad_key_lr, grad_filter_lr)
```

```python
import functools
import math

import jax
import jax.numpy as jnp
import numpy as np
from jax import lax
from jax.experimental import pallas as pl
from jax.experimental.pallas import tpu as pltpu
from jax.sharding import PartitionSpec as P

F32 = jnp.float32
BF16 = jnp.bfloat16
TOK = 128
WIDE = 256


def halves(table):
    table = np.asarray(table, np.float32)
    high = np.asarray(table.astype(BF16))
    low = (table - high.astype(np.float32)).astype(BF16)
    return high, low


def left_table(table):
    high, low = halves(table)
    return np.concatenate([high, low, high], 1)


def right_table(table):
    high, low = halves(table)
    return np.concatenate([high, high, low], 0)


def right_data(value):
    high = value.astype(BF16)
    low = (value - high.astype(F32)).astype(BF16)
    return jnp.concatenate([high, high, low], 0)


def left_data(value):
    high = value.astype(BF16)
    low = (value - high.astype(F32)).astype(BF16)
    return jnp.concatenate([high, low, high], 1)


def dot(left, right):
    return lax.dot_general(left, right, (((1,), (0,)), ((), ())), preferred_element_type=F32)


@functools.cache
def long_tables(blocks):
    total = 2 * blocks * TOK
    k = np.arange(blocks)[:, None] + 0.5
    n = np.arange(blocks)[None, :]
    m = np.arange(TOK)[None, :]
    angle = 2 * np.pi * k * n / (2 * blocks)
    first = np.concatenate([np.cos(angle), -np.sin(angle)], 0)
    last = first.T * (2.0 / total)
    turn = 2 * np.pi * k * m / total
    second = 2 * np.pi * (np.arange(TOK)[:, None] * np.arange(TOK)[None, :] % TOK) / TOK
    cos, sin = np.cos(second), np.sin(second)
    forward = np.block([[cos, -sin], [sin, cos]])
    inverse = np.block([[cos, sin], [-sin, cos]])
    return (
        left_table(first),
        np.cos(turn).astype(np.float32),
        np.sin(turn).astype(np.float32),
        right_table(forward),
        right_table(inverse),
        left_table(last),
    )


@functools.cache
def window_tables():
    f = np.arange(TOK)[:, None] + 0.5
    p = np.arange(2 * TOK)[None, :]
    angle = 2 * np.pi * f * p / (2 * TOK)
    table = np.concatenate([np.cos(angle), -np.sin(angle)], 0)
    back = table.T / TOK
    sign = np.broadcast_to((1.0 - 2.0 * (np.arange(TOK) % 2))[:, None], (TOK, TOK))
    return (
        left_table(table),
        left_table(table[:, :TOK]),
        left_table(back[:TOK]),
        left_table(back[TOK:]),
        sign.astype(np.float32),
    )


def times(a_re, a_im, b_re, b_im):
    return a_re * b_re - a_im * b_im, a_re * b_im + a_im * b_re


def conj_times(a_re, a_im, b_re, b_im):
    return a_re * b_re + a_im * b_im, a_re * b_im - a_im * b_re


def whole(shape):
    return pl.BlockSpec(shape, lambda *_: (0,) * len(shape))


def columns(rows, width):
    return pl.BlockSpec((rows, width), lambda i: (0, i))


def call(body, name, grid, in_specs, out_specs, out_shape, flops=0, nbytes=0, scratch=()):
    return pl.pallas_call(
        body,
        name=name,
        grid=grid,
        in_specs=in_specs,
        out_specs=out_specs,
        out_shape=out_shape,
        scratch_shapes=scratch,
        compiler_params=pltpu.CompilerParams(vmem_limit_bytes=48 << 20),
        cost_estimate=pl.CostEstimate(flops=flops, transcendentals=0, bytes_accessed=nbytes),
    )


def array(*shape):
    return jax.ShapeDtypeStruct(shape, F32)


def pack_body(filt_ref, grad_ref, gate_ref, out_ref):
    groups = out_ref.shape[0]
    rows = out_ref.shape[1] // 2
    out_ref[:, :rows, :] = filt_ref[...].T.reshape(groups, rows, TOK)
    out_ref[:, rows:, :] = (grad_ref[...] * gate_ref[...]).T.reshape(groups, rows, TOK)


def pack_pair(filt, grad, gate, peers):
    chans = filt.shape[1]
    rows = chans // peers
    steps = chans // WIDE
    return call(
        pack_body,
        "pack_pair",
        (steps,),
        [columns(TOK, WIDE)] * 3,
        pl.BlockSpec((peers // steps, 2 * rows, TOK), lambda i: (i, 0, 0)),
        array(peers, 2 * rows, TOK),
        nbytes=5 * chans * TOK * 4,
    )(filt, grad, gate)


def token_row(lanes_sum):
    return jnp.sum(lanes_sum.T, axis=0, keepdims=True)


def mid_forward_body(
    prev_ref, own_ref, taps_ref, layer_ref, gate_ref, win_ref, half_ref, back_ref,
    conv_ref, resid_ref, spec_ref, fspec_ref, sum_ref, acc_ref,
):
    step = pl.program_id(0)
    window = jnp.concatenate([prev_ref[...], own_ref[...]], 0)
    spec = dot(win_ref[...], right_data(window))
    fspec = dot(half_ref[...], right_data(taps_ref[...]))
    spec_ref[...] = spec
    fspec_ref[...] = fspec
    out_re, out_im = times(spec[:TOK], spec[TOK:], fspec[:TOK], fspec[TOK:])
    conv = dot(back_ref[...], right_data(jnp.concatenate([out_re, out_im], 0)))
    conv_ref[...] = conv
    resid = layer_ref[...] + gate_ref[...] * conv
    resid_ref[...] = resid
    square = resid * resid
    part = square[:, :TOK] + square[:, TOK:]

    @pl.when(step == 0)
    def _():
        acc_ref[...] = part

    @pl.when(step > 0)
    def _():
        acc_ref[...] += part

    @pl.when(step == pl.num_programs(0) - 1)
    def _():
        sum_ref[...] = jnp.broadcast_to(token_row(acc_ref[...])[None], sum_ref.shape)


def mid_forward(prev, own, taps, layer, gate, lanes):
    chans = own.shape[1]
    steps = chans // WIDE
    win, half, _, back_high, _ = window_tables()
    return call(
        mid_forward_body,
        "mid_forward",
        (steps,),
        [columns(TOK, WIDE)] * 5 + [whole(win.shape), whole(half.shape), whole(back_high.shape)],
        [
            columns(TOK, WIDE),
            columns(TOK, WIDE),
            columns(2 * TOK, WIDE),
            columns(2 * TOK, WIDE),
            whole((lanes, 8, TOK)),
        ],
        [
            array(TOK, chans),
            array(TOK, chans),
            array(2 * TOK, chans),
            array(2 * TOK, chans),
            array(lanes, 8, TOK),
        ],
        flops=2 * chans * 256 * (768 + 384 + 384),
        nbytes=11 * chans * TOK * 4,
        scratch=[pltpu.VMEM((TOK, TOK), F32)],
    )(prev, own, taps, layer, gate, win, half, back_high)


def summed_row(parts_ref):
    lanes = parts_ref.shape[0]
    total = parts_ref[0]
    for lane in range(1, lanes):
        total = total + parts_ref[lane]
    return total[:1]


def norm_body(full_width, parts_ref, resid_ref, key_ref, gain_ref, out_ref, inv_ref):
    row = lax.rsqrt(summed_row(parts_ref) / full_width + 1e-06)
    inv_ref[...] = jnp.broadcast_to(row, (TOK, TOK)).T
    value = resid_ref[...] * gain_ref[...] * key_ref[...]
    out_ref[...] = (value.T * row).reshape(out_ref.shape)


def norm_pack(parts, resid, key, gain, peers, full_width):
    chans = resid.shape[1]
    rows = chans // peers
    steps = chans // WIDE
    return call(
        functools.partial(norm_body, full_width),
        "norm_pack",
        (steps,),
        [whole(parts.shape), columns(TOK, WIDE), columns(TOK, WIDE), columns(1, WIDE)],
        [
            pl.BlockSpec((peers // steps, rows, TOK), lambda i: (i, 0, 0)),
            whole((TOK, TOK)),
        ],
        [array(peers, rows, TOK), array(TOK, TOK)],
        nbytes=3 * chans * TOK * 4,
    )(parts, resid, key, gain)


GROUP = 8


def load_group(ref, first, blocks, stride):
    return jnp.concatenate(
        [ref[pl.ds(first + c, blocks, stride=stride), :] for c in range(GROUP)], 1
    )


def store_group(ref, value, first, blocks, stride):
    for c in range(GROUP):
        ref[pl.ds(first + c, blocks, stride=stride), :] = value[:, c * TOK : (c + 1) * TOK]


def forward_group(data, first_table, cos, sin, second_table):
    blocks = cos.shape[0]
    mixed = dot(first_table, right_data(data))
    rows = []
    for c in range(GROUP):
        re = mixed[:blocks, c * TOK : (c + 1) * TOK]
        im = mixed[blocks:, c * TOK : (c + 1) * TOK]
        rows.append(jnp.concatenate([re * cos + im * sin, im * cos - re * sin], 1))
    return dot(left_data(jnp.concatenate(rows, 0)), second_table)


def inverse_group(re, im, inverse_table, cos, sin, last_table):
    blocks = cos.shape[0]
    turned = dot(left_data(jnp.concatenate([re, im], 1)), inverse_table)
    cols = []
    for c in range(GROUP):
        b_re = turned[c * blocks : (c + 1) * blocks, :TOK]
        b_im = turned[c * blocks : (c + 1) * blocks, TOK:]
        cols.append(jnp.concatenate([b_re * cos - b_im * sin, b_im * cos + b_re * sin], 0))
    return dot(last_table, right_data(jnp.concatenate(cols, 1)))


def long_back_body(
    pair_ref, first_ref, cos_ref, sin_ref, second_ref, inverse_ref, last_ref,
    out_ref, fspec_ref, gspec_ref,
):
    blocks = cos_ref.shape[0]
    chans = out_ref.shape[0] // blocks
    cos, sin = cos_ref[...], sin_ref[...]
    for group in range(chans // GROUP):
        start = group * GROUP
        rows = slice(start * blocks, (start + GROUP) * blocks)
        fspec = forward_group(
            load_group(pair_ref, start, blocks, 2 * chans),
            first_ref[...], cos, sin, second_ref[...],
        )
        gspec = forward_group(
            load_group(pair_ref, chans + start, blocks, 2 * chans),
            first_ref[...], cos, sin, second_ref[...],
        )
        fspec_ref[rows, :] = fspec
        gspec_ref[rows, :] = gspec
        re, im = conj_times(fspec[:, :TOK], fspec[:, TOK:], gspec[:, :TOK], gspec[:, TOK:])
        value = inverse_group(re, im, inverse_ref[...], cos, sin, last_ref[...])
        store_group(out_ref, value, start, blocks, chans)


def long_back(pair):
    blocks, twice, _ = pair.shape
    chans = twice // 2
    tables = long_tables(blocks)
    rows = blocks * chans
    out, fspec, gspec = call(
        long_back_body,
        "long_back",
        (),
        [pl.BlockSpec(memory_space=pltpu.VMEM)] * 7,
        [pl.BlockSpec(memory_space=pltpu.VMEM)] * 3,
        [array(rows, TOK), array(rows, 2 * TOK), array(rows, 2 * TOK)],
        flops=3 * 2 * rows * 768 * 256,
        nbytes=9 * rows * TOK * 4,
    )(pair.reshape(2 * rows, TOK), *tables)
    return out.reshape(blocks, chans, TOK), fspec, gspec


def long_rest_body(
    vals_ref, fspec_ref, gspec_ref, first_ref, cos_ref, sin_ref, second_ref, inverse_ref,
    last_ref, out_ref,
):
    blocks = cos_ref.shape[0]
    chans = vals_ref.shape[0] // blocks
    cos, sin = cos_ref[...], sin_ref[...]
    for group in range(chans // GROUP):
        start = group * GROUP
        rows = slice(start * blocks, (start + GROUP) * blocks)
        vspec = forward_group(
            load_group(vals_ref, start, blocks, chans), first_ref[...], cos, sin, second_ref[...]
        )
        v_re, v_im = vspec[:, :TOK], vspec[:, TOK:]
        re, im = times(v_re, v_im, fspec_ref[rows, :TOK], fspec_ref[rows, TOK:])
        value = inverse_group(re, im, inverse_ref[...], cos, sin, last_ref[...])
        store_group(out_ref, value, start, blocks, 2 * chans)
        re, im = conj_times(v_re, v_im, gspec_ref[rows, :TOK], gspec_ref[rows, TOK:])
        value = inverse_group(re, im, inverse_ref[...], cos, sin, last_ref[...])
        store_group(out_ref, value, chans + start, blocks, 2 * chans)


def long_rest(vals, fspec, gspec):
    blocks, chans, _ = vals.shape
    tables = long_tables(blocks)
    rows = blocks * chans
    out = call(
        long_rest_body,
        "long_rest",
        (),
        [pl.BlockSpec(memory_space=pltpu.VMEM)] * 9,
        pl.BlockSpec(memory_space=pltpu.VMEM),
        array(2 * rows, TOK),
        flops=3 * 2 * rows * 768 * 256,
        nbytes=9 * rows * TOK * 4,
    )(vals.reshape(rows, TOK), fspec, gspec, *tables)
    return out.reshape(blocks, 2 * chans, TOK)


def norm_grad_body(
    back_ref, resid_ref, key_ref, grad_ref, gain_ref, inv_ref,
    gkey_ref, base_ref, ggain_ref, sum_ref, acc_ref,
):
    step = pl.program_id(0)
    inv = jnp.concatenate([inv_ref[...]] * (WIDE // TOK), 1)
    long_grad = back_ref[...].reshape(WIDE, TOK).T
    resid = resid_ref[...]
    unit = resid * inv
    gain = gain_ref[...]
    gkey_ref[...] = long_grad * (unit * gain)
    grad_normed = long_grad * key_ref[...]
    gain_part = jnp.sum(grad_normed * unit, axis=0, keepdims=True)
    for half in range(WIDE // TOK):
        ggain_ref[pl.ds(step * (WIDE // TOK) + half, 1), :] = gain_part[
            :, half * TOK : (half + 1) * TOK
        ]
    scaled = gain * grad_normed
    base_ref[...] = grad_ref[...] + inv * scaled
    cross = scaled * resid
    part = cross[:, :TOK] + cross[:, TOK:]

    @pl.when(step == 0)
    def _():
        acc_ref[...] = part

    @pl.when(step > 0)
    def _():
        acc_ref[...] += part

    @pl.when(step == pl.num_programs(0) - 1)
    def _():
        sum_ref[...] = jnp.broadcast_to(token_row(acc_ref[...])[None], sum_ref.shape)


def norm_grad(back, resid, key, grad, gain, inv, lanes):
    chans = resid.shape[1]
    peers, rows, _ = back.shape
    steps = chans // WIDE
    return call(
        norm_grad_body,
        "norm_grad",
        (steps,),
        [
            pl.BlockSpec((peers // steps, rows, TOK), lambda i: (i, 0, 0)),
            columns(TOK, WIDE),
            columns(TOK, WIDE),
            columns(TOK, WIDE),
            columns(1, WIDE),
            whole((TOK, TOK)),
        ],
        [
            columns(TOK, WIDE),
            columns(TOK, WIDE),
            whole((chans // TOK, TOK)),
            whole((lanes, 8, TOK)),
        ],
        [
            array(TOK, chans),
            array(TOK, chans),
            array(chans // TOK, TOK),
            array(lanes, 8, TOK),
        ],
        nbytes=6 * chans * TOK * 4,
        scratch=[pltpu.VMEM((TOK, TOK), F32)],
    )(back, resid, key, grad, gain, inv)


def resid_grad_body(
    full_width, per, parts_ref, inv_ref, base_ref, resid_ref, conv_ref, gate_ref, spec_ref,
    ggain_ref, half_ref, back_ref, sign_ref,
    gresid_ref, gquery_ref, gconv_ref, pieces_ref,
):
    step = pl.program_id(0)
    mean = jnp.broadcast_to(summed_row(parts_ref) / full_width, (TOK, TOK)).T
    inv = inv_ref[...]
    scale = jnp.concatenate([inv * inv * inv * mean] * (WIDE // TOK), 1)
    gresid = base_ref[...] - resid_ref[...] * scale
    gresid_ref[...] = gresid
    gquery_ref[...] = gresid * conv_ref[...]
    gconv = gresid * gate_ref[...]
    gconv_ref[...] = gconv
    low = dot(half_ref[...], right_data(gconv))
    sign = jnp.concatenate([sign_ref[...]] * (WIDE // TOK), 1)
    re, im = conj_times(spec_ref[:TOK, :], spec_ref[TOK:, :], sign * low[TOK:], -sign * low[:TOK])
    part = dot(back_ref[...], right_data(jnp.concatenate([re, im], 0)))
    per_step = WIDE // TOK
    slot = step * per_step // per
    base_row = (step * per_step) % per * 8
    stride = ggain_ref.shape[0] // per
    for tap in range(TOK // 8):
        for half in range(per_step):
            pieces_ref[
                tap * stride + slot, pl.ds(pl.multiple_of(base_row + half * 8, 8), 8), :
            ] = part[tap * 8 : tap * 8 + 8, half * TOK : (half + 1) * TOK]

    @pl.when(step == 0)
    def _():
        pieces_ref[:, per * 8 :, :] = jnp.broadcast_to(
            ggain_ref[...][None], (pieces_ref.shape[0],) + ggain_ref.shape
        )


def resid_grad(parts, inv, base, resid, conv, gate, spec, ggain, peers, full_width):
    chans = resid.shape[1]
    steps = chans // WIDE
    per = (TOK // 8) * (chans // TOK) // peers
    rows = per * 8 + ggain.shape[0]
    _, half, back_low, _, sign = window_tables()
    return call(
        functools.partial(resid_grad_body, full_width, per),
        "resid_grad",
        (steps,),
        [
            whole(parts.shape),
            whole((TOK, TOK)),
            columns(TOK, WIDE),
            columns(TOK, WIDE),
            columns(TOK, WIDE),
            columns(TOK, WIDE),
            columns(2 * TOK, WIDE),
            whole(ggain.shape),
            whole(half.shape),
            whole(back_low.shape),
            whole(sign.shape),
        ],
        [columns(TOK, WIDE)] * 3 + [whole((peers, rows, TOK))],
        [array(TOK, chans)] * 3 + [array(peers, rows, TOK)],
        flops=2 * chans * (256 * 384 + 128 * 768),
        nbytes=10 * chans * TOK * 4,
    )(parts, inv, base, resid, conv, gate, spec, ggain, half, back_low, sign)


def mid_grad_body(
    own_ref, next_ref, fspec_ref, gresid_ref, layer_ref, key_ref, win_ref, back_ref,
    gkey_ref, gin_ref,
):
    window = jnp.concatenate([own_ref[...], next_ref[...]], 0)
    spec = dot(win_ref[...], right_data(window))
    re, im = conj_times(fspec_ref[:TOK, :], fspec_ref[TOK:, :], spec[:TOK], spec[TOK:])
    mixed = dot(back_ref[...], right_data(jnp.concatenate([re, im], 0)))
    gkey_ref[...] = mixed * layer_ref[...]
    gin_ref[...] = gresid_ref[...] + mixed * key_ref[...]


def mid_grad(own, following, fspec, gresid, layer, key):
    chans = own.shape[1]
    win, _, back_low, _, _ = window_tables()
    return call(
        mid_grad_body,
        "mid_grad",
        (chans // WIDE,),
        [
            columns(TOK, WIDE),
            columns(TOK, WIDE),
            columns(2 * TOK, WIDE),
            columns(TOK, WIDE),
            columns(TOK, WIDE),
            columns(TOK, WIDE),
            whole(win.shape),
            whole(back_low.shape),
        ],
        [columns(TOK, WIDE)] * 2,
        [array(TOK, chans)] * 2,
        flops=2 * chans * (256 * 768 + 128 * 768),
        nbytes=9 * chans * TOK * 4,
    )(own, following, fspec, gresid, layer, key, win, back_low)


def unpack_body(pair_ref, grad_ref, gquery_ref, gfilt_ref):
    rows = pair_ref.shape[1] // 2
    gquery_ref[...] = grad_ref[...] * pair_ref[:, :rows, :].reshape(WIDE, TOK).T
    gfilt_ref[...] = pair_ref[:, rows:, :].reshape(WIDE, TOK).T


def unpack_pair(pair, grad):
    chans = grad.shape[1]
    peers, twice, _ = pair.shape
    steps = chans // WIDE
    return call(
        unpack_body,
        "unpack_pair",
        (steps,),
        [
            pl.BlockSpec((peers // steps, twice, TOK), lambda i: (i, 0, 0)),
            columns(TOK, WIDE),
        ],
        [columns(TOK, WIDE)] * 2,
        [array(TOK, chans)] * 2,
        nbytes=5 * chans * TOK * 4,
    )(pair, grad)


def fold_body(pieces_ref, copies_ref, ggain_ref):
    total = jnp.sum(pieces_ref[...], axis=0)
    rows = copies_ref.shape[1]
    copies_ref[...] = jnp.broadcast_to(total[None, :rows], copies_ref.shape)
    ggain_ref[...] = total[rows:]


def fold_pieces(pieces, gain_rows):
    peers, rows, _ = pieces.shape
    kept = rows - gain_rows
    return call(
        fold_body,
        "fold_pieces",
        (),
        [pl.BlockSpec(memory_space=pltpu.VMEM)],
        [pl.BlockSpec(memory_space=pltpu.VMEM)] * 2,
        [array(peers, kept, TOK), array(gain_rows, TOK)],
        nbytes=2 * peers * rows * TOK * 4,
    )(pieces)


def exchange(value, axis):
    return lax.all_to_all(value, axis, split_axis=0, concat_axis=0, tiled=True)


def shifted(block, axis, by):
    peers = lax.axis_size(axis)
    pairs = [(i, i + by) for i in range(peers) if 0 <= i + by < peers]
    return lax.ppermute(block, axis, pairs)


def shards(layer_in, query_mr, key_mr, query_lr, key_lr, filter_mr, filter_lr, norm_gain, out_grad):
    chans = layer_in.shape[1]
    peers = lax.axis_size("ctx")
    lanes = lax.axis_size("chan")
    full_width = float(chans * lanes)
    gain = norm_gain[None, :]
    mixed_in = key_mr * layer_in
    preceding = shifted(mixed_in, "ctx", 1)
    pair = exchange(pack_pair(filter_lr, out_grad, query_lr, peers), "ctx")
    conv_mr, residual, spec, fspec_mr, squares = mid_forward(
        preceding, mixed_in, filter_mr, layer_in, query_mr, lanes
    )
    squares = exchange(squares, "chan")
    values, inv = norm_pack(squares, residual, key_lr, gain, peers, full_width)
    back, fspec, gspec = long_back(pair)
    back = exchange(back, "ctx")
    values = exchange(values, "ctx")
    grad_key_lr, base, gain_part, cross = norm_grad(
        back, residual, key_lr, out_grad, gain, inv, lanes
    )
    cross = exchange(cross, "chan")
    grad_resid, grad_query_mr, grad_conv_mr, pieces = resid_grad(
        cross, inv, base, residual, conv_mr, query_mr, spec, gain_part, peers, full_width
    )
    following = shifted(grad_conv_mr, "ctx", -1)
    pieces = exchange(pieces, "ctx")
    rest = exchange(long_rest(values, fspec, gspec), "ctx")
    copies, gain_sum = fold_pieces(pieces, chans // TOK)
    taps = exchange(copies, "ctx")
    grad_key_mr, grad_in = mid_grad(
        grad_conv_mr, following, fspec_mr, grad_resid, layer_in, key_mr
    )
    grad_query_lr, grad_filter_lr = unpack_pair(rest, out_grad)
    tap_blocks = TOK // 8
    grad_filter_mr = (
        taps.reshape(tap_blocks, chans // TOK, 8, TOK).transpose(0, 2, 1, 3).reshape(TOK, chans)
    )
    return (
        grad_in,
        grad_query_mr,
        grad_key_mr,
        grad_filter_mr,
        gain_sum.reshape(chans),
        grad_query_lr,
        grad_key_lr,
        grad_filter_lr,
    )


def solution(mesh):
    rows = P("ctx", "chan")
    in_specs = (rows, rows, rows, rows, rows, P(None, "chan"), rows, P("chan"), rows)
    out_specs = (rows, rows, rows, P(None, "chan"), P("chan"), rows, rows, rows)
    return jax.shard_map(shards, mesh=mesh, in_specs=in_specs, out_specs=out_specs, check_vma=False)
```
